32 devices in a mesh: tm: 16 (over z, x, core), comp: 2 (over y).
Axes of the slice: x: 2, y: 2, z: 4, core: 2. Of those that a mesh axis runs over, the one named last changes fastest.
Arguments:
- velocities: bfloat16 [4096, 3, 1024], P('tm', None, 'comp'), may hold values from -6 to 6
- atom_mask: int32 [1024], P('comp'), may hold values 0 or 1
- valid_frames: int32 [1], replicated, may hold values from 3840 to 4096
Outputs:
- correlation: float32 [256, 1024], P('tm', 'comp')
- average: float32 [256], P('tm')
The draws below stay inside these ranges and needn't reach their ends.
All inputs are finite; a program needn't handle non-finite values. No bound on the sum of `atom_mask` on one device may be relied on, other than what follows from the above.
Results may differ from the reference program's by a relative error of at most 0.0003.
Values may be sent and summed in bfloat16 or wider, within the bound.
A program may use at most 64 MiB of HBM per device.

```python
import math
import jax
import jax.numpy as jnp
from jax import lax

LAGS = 256
FR_DEV = 256
FRAMES = 4096
ATOMS = 1024


def draw_velocities(key, part):
    keys = jax.random.split(key, 5)
    drift = 0.6 * jax.random.normal(keys[0], (1, 3, ATOMS), jnp.float32)
    amplitude = jax.random.uniform(keys[1], (1, 3, ATOMS), jnp.float32, 0.7, 1.3)
    noise = 0.5 * jax.random.normal(keys[2], (FRAMES, 3, ATOMS), jnp.float32)
    frequency = jax.random.randint(keys[3], (ATOMS,), FRAMES // 32, 2 * FRAMES // 5 + 1, jnp.int32)
    phase = jax.random.uniform(keys[4], (1, 3, ATOMS), jnp.float32, -math.pi, math.pi)
    ticks = jnp.arange(FRAMES, dtype=jnp.int32)[:, None] * frequency[None, :] % FRAMES
    angle = ticks.astype(jnp.float32) * (2.0 * math.pi / FRAMES)
    values = drift + amplitude * jnp.cos(angle[:, None, :] + phase) + noise
    values = jnp.clip(values, -6.0, 6.0)
    return values.astype(jnp.bfloat16)


def place_ends(entries, stream_key, low, high):
    longest = entries.shape.index(max(entries.shape))
    spots = []
    for shift in (0, 1):
        where = [jax.random.randint(jax.random.fold_in(stream_key, axis), (), 0, length) for axis, length in enumerate(entries.shape)]
        where[longest] = (where[longest] + shift) % entries.shape[longest]
        spots.append(tuple(where))
    return entries.at[spots[0]].set(low).at[spots[1]].set(high)


def setup_inputs(seed: int = 0) -> dict:
    seeds = jax.random.split(jax.random.key(seed), 4)
    return {
        "velocities": draw_velocities(jax.random.fold_in(seeds[3], 71), 0),
        "atom_mask": place_ends((jax.random.randint(seeds[1], (ATOMS,), 0, 8) < 7).astype(jnp.int32), jax.random.fold_in(seeds[1], 1), 0, 1),
        "valid_frames": jax.random.randint(seeds[2], (1,), FRAMES - 2 * FR_DEV + LAGS, FRAMES + 1).astype(jnp.int32),
    }


def reference(velocities, atom_mask, valid_frames):
    frame_count = velocities.shape[0]
    last_valid = valid_frames[0]
    in_range = jnp.arange(frame_count, dtype=jnp.int32) < last_valid
    clean = jnp.where(in_range[:, None, None], velocities, jnp.zeros_like(velocities))
    padded = jnp.concatenate([clean, jnp.zeros((LAGS, clean.shape[1], clean.shape[2]), clean.dtype)], 0)

    def per_offset(offset):
        shifted = lax.dynamic_slice_in_dim(padded, offset, frame_count, 0)
        return jnp.sum(clean.astype(jnp.float32) * shifted.astype(jnp.float32), axis=(0, 1))

    lag_sums = lax.map(per_offset, jnp.arange(LAGS, dtype=jnp.int32))
    anchors = (last_valid - jnp.arange(LAGS, dtype=jnp.int32)).astype(jnp.float32)
    atom_weight = atom_mask.astype(jnp.float32)
    correlation = atom_weight[None, :] * lag_sums / anchors[:, None]
    average = jnp.sum(correlation, axis=1) / jnp.maximum(jnp.sum(atom_weight), 1.0)
    return correlation, average
```

```python
import functools
import math

import jax
import jax.numpy as jnp
import numpy as np
from jax import lax
from jax.sharding import PartitionSpec as P

LAGS = 256


def split_bf16(table):
    high = table.astype(np.float32).astype(jnp.bfloat16)
    low = (table - high.astype(np.float64)).astype(np.float32).astype(jnp.bfloat16)
    return high, low


@functools.lru_cache
def tables(frame_count):
    length = 2 * frame_count
    bins = np.arange(frame_count, dtype=np.int64)[:, None]
    own = np.arange(frame_count, dtype=np.int64)[None, :]
    angle = (((2 * bins + 1) * own) % (2 * length)) * (math.pi / length)
    forward = np.concatenate([np.cos(angle), np.sin(angle)], 0)
    lags = np.arange(LAGS, dtype=np.int64)[:, None]
    angle = (((2 * bins.T + 1) * lags) % (2 * length)) * (math.pi / length)
    inverse = np.concatenate([np.cos(angle), -np.sin(angle)], 1) * (2.0 / length)
    sign = np.where(bins % 2 == 0, 1.0, -1.0).astype(np.float32)
    return split_bf16(forward), split_bf16(inverse), sign


def dot(a, b):
    return jnp.dot(a, b, preferred_element_type=jnp.float32)


def body(velocities, atom_mask, valid_frames):
    frame_count, xyz_count, atom_count = velocities.shape
    last_valid = valid_frames[0]
    count = lax.axis_size("tm")
    following = lax.ppermute(velocities, "tm", [(s, s - 1) for s in range(1, count)])
    anchor_frame = lax.axis_index("tm") * frame_count
    frame = anchor_frame + jnp.arange(frame_count, dtype=jnp.int32)
    (fwd_hi, fwd_lo), (inv_hi, inv_lo), sign = tables(frame_count)

    def spectrum(block, frames, k):
        x = jnp.where((frames < last_valid)[:, None], block[:, k, :], jnp.zeros((), block.dtype))
        y = dot(fwd_hi, x) + dot(fwd_lo, x)
        return y[:frame_count], y[frame_count:]

    real = imag = 0.0
    for k in range(xyz_count):
        ac, as_ = spectrum(velocities, frame, k)
        nc, ns = spectrum(following, frame + frame_count, k)
        nc, ns = -sign * ns, sign * nc
        real = real + ac * (ac + nc) + as_ * (as_ + ns)
        imag = imag + as_ * nc - ac * ns
    power = jnp.concatenate([real, imag], 0)
    rounded = lax.reduce_precision(power, 8, 7)
    p_hi = rounded.astype(jnp.bfloat16)
    p_lo = (power - rounded).astype(jnp.bfloat16)
    lag_sums = dot(inv_hi, p_hi) + (dot(inv_hi, p_lo) + dot(inv_lo, p_hi))

    per_device = LAGS // count
    first_lag = lax.axis_index("tm") * per_device
    own_rows = lax.psum_scatter(lag_sums, "tm", scatter_dimension=0, tiled=True)
    lag_index = first_lag + jnp.arange(per_device, dtype=jnp.int32)
    anchors = (last_valid - lag_index).astype(jnp.float32)
    atom_weight = atom_mask.astype(jnp.float32)
    correlation = atom_weight[None, :] * own_rows / anchors[:, None]
    total_corr, real_atoms = lax.psum((jnp.sum(correlation, axis=1), jnp.sum(atom_weight)), "comp")
    average = total_corr / jnp.maximum(real_atoms, 1.0)
    return (correlation, average)


def solution(mesh):
    return jax.shard_map(
        body,
        mesh=mesh,
        in_specs=(P("tm", None, "comp"), P("comp"), P()),
        out_specs=(P("tm", "comp"), P("tm")),
        check_vma=False,
    )
```

```python
import functools
import math

import jax
import jax.numpy as jnp
import numpy as np
from jax import lax
from jax.experimental import pallas as pl
from jax.experimental.pallas import tpu as pltpu
from jax.sharding import PartitionSpec as P

LAGS = 256
CHUNKS = 2
MESH = pl.DeviceIdType.MESH


def split_bf16(table):
    high = table.astype(np.float32).astype(jnp.bfloat16)
    low = (table - high.astype(np.float64)).astype(np.float32).astype(jnp.bfloat16)
    return high, low


@functools.lru_cache
def tables(frame_count, count):
    length = 2 * frame_count
    bins = np.arange(frame_count, dtype=np.int64)[:, None]
    own = np.arange(frame_count, dtype=np.int64)[None, :]
    angle = (((2 * bins + 1) * own) % (2 * length)) * (math.pi / length)
    forward = np.concatenate([np.cos(angle), np.sin(angle)], 0)
    per = LAGS // count
    lags = np.arange(LAGS, dtype=np.int64).reshape(count // 4, 2, 2, per)
    lags = lags.transpose(2, 1, 0, 3).reshape(LAGS, 1)
    angle = (((2 * bins.T + 1) * lags) % (2 * length)) * (math.pi / length)
    inverse = np.concatenate([np.cos(angle), -np.sin(angle)], 1) * (2.0 / length)
    return split_bf16(forward) + split_bf16(inverse)


def dot(a, b):
    return jnp.dot(a, b, preferred_element_type=jnp.float32)


def kernel(
    n, groups,
    valid_ref, vel_ref, mask_ref, fwd_hi, fwd_lo, inv_hi, inv_lo,
    corr_ref, avg_ref,
    nxt, spec, part, pair_in, q_ref, x_in, r_ref, z_in, comp_out, comp_in,
    halo_s, halo_r, pair_s, pair_r, x_s, x_r, z_s, z_r, comp_s, comp_r,
):
    xyz, frames, atoms = vel_ref.shape
    width = atoms // CHUNKS
    nz = n // 4
    per = LAGS // n
    me = lax.axis_index("tm")
    mine = lax.axis_index("comp")
    core = lax.rem(me, 2)
    xpos = lax.rem(me // 2, 2)
    zpos = me // 4
    pair = me + 1 - 2 * core
    across = me + 2 - 4 * xpos
    left = lax.rem(me + n - 1, n)
    right = lax.rem(me + 1, n)

    def along_z(d):
        return lax.rem(zpos + d, nz)

    def z_device(d):
        return along_z(d) * 4 + lax.rem(me, 4)

    barrier = pltpu.get_barrier_semaphore()
    for device in [left, right, pair, across] + [z_device(d) for d in range(1, nz)]:
        pl.semaphore_signal(barrier, inc=1, device_id={"tm": device}, device_id_type=MESH)
    for d in range(1, groups):
        pl.semaphore_signal(
            barrier, inc=1, device_id={"comp": lax.rem(mine + d, groups)}, device_id_type=MESH
        )
    pl.semaphore_wait(barrier, 4 + (nz - 1) + (groups - 1))

    def remote(src, dst, send, recv, device):
        return pltpu.make_async_remote_copy(
            src_ref=src, dst_ref=dst, send_sem=send, recv_sem=recv,
            device_id=device, device_id_type=MESH,
        )

    def halo(c, k):
        lanes = pl.ds(c * width, width)
        return remote(
            vel_ref.at[k, :, lanes], nxt.at[c, k], halo_s.at[c, k], halo_r.at[c, k], {"tm": left}
        )

    @pl.when(me > 0)
    def _():
        for c in range(CHUNKS):
            for k in range(xyz):
                halo(c, k).start()

    @pl.when(me == n - 1)
    def _():
        nxt[...] = jnp.zeros_like(nxt)

    last_valid = valid_ref[0]
    row = lax.broadcasted_iota(jnp.int32, (frames, width), 0) + me * frames
    keep_own = jnp.where(row < last_valid, 1.0, 0.0).astype(jnp.bfloat16)
    keep_nxt = jnp.where(row + frames < last_valid, 1.0, 0.0).astype(jnp.bfloat16)
    bins = lax.broadcasted_iota(jnp.int32, (frames, width), 0)
    sign = jnp.where(lax.rem(bins, 2) == 0, 1.0, -1.0)

    def spectrum(x):
        return dot(fwd_hi[...], x) + dot(fwd_lo[...], x)

    for c in range(CHUNKS):
        for k in range(xyz):
            spec[c, k] = spectrum(vel_ref[k, :, c * width : (c + 1) * width] * keep_own)

    def pair_copy(c):
        return remote(part.at[c, 1 - core], pair_in.at[c], pair_s.at[c], pair_r.at[c], {"tm": pair})

    def x_copy(c):
        return remote(q_ref.at[c, 1 - xpos], x_in.at[c], x_s.at[c], x_r.at[c], {"tm": across})

    def z_copy(c, d):
        return remote(
            r_ref.at[c, along_z(d)], z_in.at[c, d - 1], z_s.at[c, d - 1], z_r.at[c, d - 1],
            {"tm": z_device(d)},
        )

    def correlate(c):
        real = imag = 0.0
        for k in range(xyz):
            @pl.when(me < n - 1)
            def _():
                halo(c, k).wait_recv()

            other = spectrum(nxt[c, k] * keep_nxt)
            nc, ns = -sign * other[frames:], sign * other[:frames]
            ac, as_ = spec[c, k, :frames], spec[c, k, frames:]
            real = real + ac * (ac + nc) + as_ * (as_ + ns)
            imag = imag + as_ * nc - ac * ns
        power = jnp.concatenate([real, imag], 0)
        high = power.astype(jnp.bfloat16)
        low = (power - high.astype(jnp.float32)).astype(jnp.bfloat16)
        sums = dot(inv_hi[...], high) + (dot(inv_hi[...], low) + dot(inv_lo[...], high))
        part[c] = sums.reshape(part.shape[1:])
        pair_copy(c).start()

    def after_pair(c):
        pair_copy(c).wait_recv()
        q_ref[c] = part[c, core] + pair_in[c]
        x_copy(c).start()

    def after_x(c):
        x_copy(c).wait_recv()
        r_ref[c] = q_ref[c, xpos] + x_in[c]
        for d in range(1, nz):
            z_copy(c, d).start()

    correlate(0)
    after_pair(0)
    for c in range(1, CHUNKS):
        correlate(c)
        after_x(c - 1)
        after_pair(c)
    after_x(CHUNKS - 1)

    lag = me * per + lax.broadcasted_iota(jnp.int32, (per, width), 0)
    anchors = (last_valid - lag).astype(jnp.float32)
    weight = mask_ref[...].astype(jnp.float32)
    total = jnp.zeros((per, 1), jnp.float32)
    for c in range(CHUNKS):
        rows = r_ref[c, zpos]
        for d in range(1, nz):
            z_copy(c, d).wait_recv()
            rows = rows + z_in[c, d - 1]
        lanes = slice(c * width, (c + 1) * width)
        corr = weight[:, lanes] * rows / anchors
        corr_ref[:, lanes] = corr
        total = total + jnp.sum(corr, axis=1, keepdims=True)
    real_atoms = jnp.sum(weight, axis=1, keepdims=True)
    comp_out[:per] = jnp.broadcast_to(total, (per, 128))
    comp_out[per:] = jnp.broadcast_to(real_atoms, (8, 128))

    def comp_copy(d):
        return remote(
            comp_out, comp_in.at[d - 1], comp_s.at[d - 1], comp_r.at[d - 1],
            {"comp": lax.rem(mine + d, groups)},
        )

    for d in range(1, groups):
        comp_copy(d).start()
    both = comp_out[...]
    for d in range(1, groups):
        comp_copy(d).wait_recv()
        both = both + comp_in[d - 1]
    avg_ref[...] = both[:per] / jnp.maximum(both[per : per + 1], 1.0)

    @pl.when(me > 0)
    def _():
        for c in range(CHUNKS):
            for k in range(xyz):
                halo(c, k).wait_send()

    for c in range(CHUNKS):
        pair_copy(c).wait_send()
        x_copy(c).wait_send()
        for d in range(1, nz):
            z_copy(c, d).wait_send()
    for d in range(1, groups):
        comp_copy(d).wait_send()


def body(velocities, atom_mask, valid_frames):
    frames, xyz, atoms = velocities.shape
    n = lax.axis_size("tm")
    groups = lax.axis_size("comp")
    nz, per, width = n // 4, LAGS // n, atoms // CHUNKS
    f32 = jnp.float32
    vmem = pl.BlockSpec(memory_space=pltpu.VMEM)
    dma = pltpu.SemaphoreType.DMA
    correlation, average = pl.pallas_call(
        functools.partial(kernel, n, groups),
        out_shape=(
            jax.ShapeDtypeStruct((per, atoms), f32),
            jax.ShapeDtypeStruct((per, 128), f32),
        ),
        in_specs=[pl.BlockSpec(memory_space=pltpu.SMEM)] + [vmem] * 6,
        out_specs=(vmem, vmem),
        scratch_shapes=[
            pltpu.VMEM((CHUNKS, xyz, frames, width), jnp.bfloat16),
            pltpu.VMEM((CHUNKS, xyz, 2 * frames, width), f32),
            pltpu.VMEM((CHUNKS, 2, 2, nz, per, width), f32),
            pltpu.VMEM((CHUNKS, 2, nz, per, width), f32),
            pltpu.VMEM((CHUNKS, 2, nz, per, width), f32),
            pltpu.VMEM((CHUNKS, nz, per, width), f32),
            pltpu.VMEM((CHUNKS, nz, per, width), f32),
            pltpu.VMEM((CHUNKS, nz - 1, per, width), f32),
            pltpu.VMEM((per + 8, 128), f32),
            pltpu.VMEM((groups - 1, per + 8, 128), f32),
            dma((CHUNKS, xyz)), dma((CHUNKS, xyz)),
            dma((CHUNKS,)), dma((CHUNKS,)),
            dma((CHUNKS,)), dma((CHUNKS,)),
            dma((CHUNKS, nz - 1)), dma((CHUNKS, nz - 1)),
            dma((groups - 1,)), dma((groups - 1,)),
        ],
        compiler_params=pltpu.CompilerParams(
            collective_id=0, has_side_effects=True, vmem_limit_bytes=40 * 1024 * 1024
        ),
    )(
        valid_frames, jnp.transpose(velocities, (1, 0, 2)), atom_mask[None, :],
        *tables(frames, n),
    )
    return correlation, average[:, 0]


def solution(mesh):
    return jax.shard_map(
        body,
        mesh=mesh,
        in_specs=(P("tm", None, "comp"), P("comp"), P()),
        out_specs=(P("tm", "comp"), P("tm")),
        check_vma=False,
    )
```

```python
import functools
import math

import jax
import jax.numpy as jnp
import numpy as np
from jax import lax
from jax.experimental import pallas as pl
from jax.experimental.pallas import tpu as pltpu
from jax.sharding import PartitionSpec as P

LAGS = 256
CHUNKS = 4
MESH = pl.DeviceIdType.MESH


def split_bf16(table):
    high = table.astype(np.float32).astype(jnp.bfloat16)
    low = (table - high.astype(np.float64)).astype(np.float32).astype(jnp.bfloat16)
    return high, low


@functools.lru_cache
def tables(frame_count, count):
    length = 2 * frame_count
    bins = np.arange(frame_count, dtype=np.int64)[:, None]
    own = np.arange(frame_count, dtype=np.int64)[None, :]
    angle = (((2 * bins + 1) * own) % (2 * length)) * (math.pi / length)
    forward = np.concatenate([np.cos(angle), np.sin(angle)], 0)
    per = LAGS // count
    lags = np.arange(LAGS, dtype=np.int64).reshape(count // 4, 2, 2, per)
    lags = lags.transpose(2, 0, 1, 3).reshape(LAGS, 1)
    angle = (((2 * bins.T + 1) * lags) % (2 * length)) * (math.pi / length)
    inverse = np.concatenate([np.cos(angle), -np.sin(angle)], 1) * (2.0 / length)
    return split_bf16(forward) + split_bf16(inverse)


def dot(a, b):
    return jnp.dot(a, b, preferred_element_type=jnp.float32)


def kernel(
    n, groups,
    valid_ref, vel_hbm, mask_ref, fwd_hi_hbm, fwd_lo_hbm, inv_hi_hbm, inv_lo_hbm,
    corr_ref, avg_ref,
    vel_ref, fwd_hi, fwd_lo, inv_hi, inv_lo,
    nxt, spec, part, pair_in, q_ref, z_in, r_ref, x_in, comp_out, comp_in,
    load_s, halo_s, halo_r, pair_s, pair_r, z_s, z_r, x_s, x_r, comp_s, comp_r,
):
    xyz, frames, atoms = vel_ref.shape
    width = atoms // CHUNKS
    nz = n // 4
    per = LAGS // n
    me = lax.axis_index("tm")
    mine = lax.axis_index("comp")
    core = lax.rem(me, 2)
    xpos = lax.rem(me // 2, 2)
    zpos = me // 4
    pair = me + 1 - 2 * core
    across = me + 2 - 4 * xpos
    left = lax.rem(me + n - 1, n)
    right = lax.rem(me + 1, n)

    loads = [
        pltpu.make_async_copy(src, dst, load_s.at[i])
        for i, (src, dst) in enumerate(
            [
                (fwd_hi_hbm, fwd_hi), (fwd_lo_hbm, fwd_lo), (vel_hbm, vel_ref),
                (inv_hi_hbm, inv_hi), (inv_lo_hbm, inv_lo),
            ]
        )
    ]
    for load in loads:
        load.start()

    def along_z(d):
        return lax.rem(zpos + d, nz)

    def z_device(d):
        return along_z(d) * 4 + lax.rem(me, 4)

    def group(d):
        return lax.rem(mine + d, groups)

    barrier = pltpu.get_barrier_semaphore()
    for device in [left, right, pair, across] + [z_device(d) for d in range(1, nz)]:
        pl.semaphore_signal(barrier, inc=1, device_id={"tm": device}, device_id_type=MESH)
    for d in range(1, groups):
        for device in (me, across):
            pl.semaphore_signal(
                barrier, inc=1, device_id={"comp": group(d), "tm": device}, device_id_type=MESH
            )
    pl.semaphore_wait(barrier, 4 + (nz - 1) + 2 * (groups - 1))

    def remote(src, dst, send, recv, device):
        return pltpu.make_async_remote_copy(
            src_ref=src, dst_ref=dst, send_sem=send, recv_sem=recv,
            device_id=device, device_id_type=MESH,
        )

    def halo(c, k):
        lanes = pl.ds(c * width, width)
        return remote(
            vel_hbm.at[k, :, lanes], nxt.at[c, k], halo_s.at[c, k], halo_r.at[c, k], {"tm": left}
        )

    @pl.when(me > 0)
    def _():
        for c in range(CHUNKS):
            for k in range(xyz):
                halo(c, k).start()

    @pl.when(me == n - 1)
    def _():
        nxt[...] = jnp.zeros_like(nxt)

    last_valid = valid_ref[0]

    def keep(offset, lanes):
        row = lax.broadcasted_iota(jnp.int32, (frames, lanes), 0) + (me * frames + offset)
        return jnp.where(row < last_valid, 1.0, 0.0).astype(jnp.bfloat16)

    bins = lax.broadcasted_iota(jnp.int32, (frames, width), 0)
    sign = jnp.where(lax.rem(bins, 2) == 0, 1.0, -1.0)
    weight = mask_ref[...].astype(jnp.float32)

    def spectrum(x):
        return dot(fwd_hi[...], x) + dot(fwd_lo[...], x)

    for load in loads[:3]:
        load.wait()
    step = 2 if CHUNKS % 2 == 0 else 1
    keep_own = keep(0, step * width)
    for c in range(0, CHUNKS, step):
        for k in range(xyz):
            both = spectrum(vel_ref[k, :, c * width : (c + step) * width] * keep_own)
            for j in range(step):
                spec[c + j, k] = both[:, j * width : (j + 1) * width]
    for load in loads[3:]:
        load.wait()

    keep_nxt = keep(frames, width)

    def pair_copy(c):
        return remote(part.at[c, 1 - core], pair_in.at[c], pair_s.at[c], pair_r.at[c], {"tm": pair})

    def z_copy(c, d):
        return remote(
            q_ref.at[c, along_z(d)], z_in.at[c, d - 1], z_s.at[c, d - 1], z_r.at[c, d - 1],
            {"tm": z_device(d)},
        )

    def x_copy(c):
        return remote(r_ref.at[c, 1 - xpos], x_in.at[c], x_s.at[c], x_r.at[c], {"tm": across})

    def lanes_of(c):
        return slice(c * width, (c + 1) * width)

    def atom_sum(c, rows):
        return jnp.sum(weight[:, lanes_of(c)] * rows, axis=1, keepdims=True)

    def after_pair(c):
        pair_copy(c).wait_recv()
        q_ref[c] = part[c, core] + pair_in[c]
        for d in range(1, nz):
            z_copy(c, d).start()

    totals = {}

    def after_z(c):
        rows = q_ref[c, zpos]
        for d in range(1, nz):
            z_copy(c, d).wait_recv()
            rows = rows + z_in[c, d - 1]
        r_ref[c] = rows
        x_copy(c).start()
        totals[c] = (atom_sum(c, r_ref[c, xpos]), atom_sum(c, r_ref[c, 1 - xpos]))

    def correlate(c):
        real = imag = 0.0
        for k in range(xyz):
            if k == 1 and c >= 1:
                after_pair(c - 1)
            if k == xyz - 1 and c >= 2:
                after_z(c - 2)

            @pl.when(me < n - 1)
            def _():
                halo(c, k).wait_recv()

            other = spectrum(nxt[c, k] * keep_nxt)
            nc, ns = -sign * other[frames:], sign * other[:frames]
            ac, as_ = spec[c, k, :frames], spec[c, k, frames:]
            real = real + ac * (ac + nc) + as_ * (as_ + ns)
            imag = imag + as_ * nc - ac * ns
        power = jnp.concatenate([real, imag], 0)
        high = power.astype(jnp.bfloat16)
        low = (power - high.astype(jnp.float32)).astype(jnp.bfloat16)
        sums = dot(inv_hi[...], high) + (dot(inv_hi[...], low) + dot(inv_lo[...], high))
        part[c] = sums.reshape(part.shape[1:])
        pair_copy(c).start()

    for c in range(CHUNKS):
        correlate(c)
    after_pair(CHUNKS - 1)
    if CHUNKS > 1:
        after_z(CHUNKS - 2)
    after_z(CHUNKS - 1)

    total = sum(t[0] for t in totals.values())
    beside = sum(t[1] for t in totals.values())
    real_atoms = jnp.sum(weight, axis=1, keepdims=True)
    comp_out[0, :per] = jnp.broadcast_to(total, (per, 128))
    comp_out[0, per:] = jnp.broadcast_to(real_atoms, (8, 128))
    comp_out[1, :per] = jnp.broadcast_to(beside, (per, 128))
    comp_out[1, per:] = jnp.zeros((8, 128), jnp.float32)

    def comp_copy(side, d):
        return remote(
            comp_out.at[side], comp_in.at[side, d - 1], comp_s.at[side, d - 1],
            comp_r.at[side, d - 1], {"comp": group(d), "tm": (me, across)[side]},
        )

    for side in range(2):
        for d in range(1, groups):
            comp_copy(side, d).start()

    lag = me * per + lax.broadcasted_iota(jnp.int32, (per, width), 0)
    anchors = (last_valid - lag).astype(jnp.float32)
    for c in range(CHUNKS):
        kept = r_ref[c, xpos]
        x_copy(c).wait_recv()
        arrived = x_in[c]
        corr_ref[:, lanes_of(c)] = weight[:, lanes_of(c)] * (kept + arrived) / anchors
        total = total + atom_sum(c, arrived)
    sums = jnp.broadcast_to(total, (per, 128))
    count = jnp.broadcast_to(real_atoms, (8, 128))
    for side in range(2):
        for d in range(1, groups):
            comp_copy(side, d).wait_recv()
            sums = sums + comp_in[side, d - 1, :per]
            count = count + comp_in[side, d - 1, per:]
    avg_ref[...] = sums / anchors[:, :128] / jnp.maximum(count[:1], 1.0)

    @pl.when(me > 0)
    def _():
        for c in range(CHUNKS):
            for k in range(xyz):
                halo(c, k).wait_send()

    for c in range(CHUNKS):
        pair_copy(c).wait_send()
        x_copy(c).wait_send()
        for d in range(1, nz):
            z_copy(c, d).wait_send()
    for side in range(2):
        for d in range(1, groups):
            comp_copy(side, d).wait_send()


def body(velocities, atom_mask, valid_frames):
    frames, xyz, atoms = velocities.shape
    n = lax.axis_size("tm")
    groups = lax.axis_size("comp")
    nz, per, width = n // 4, LAGS // n, atoms // CHUNKS
    f32, bf16 = jnp.float32, jnp.bfloat16
    vmem = pl.BlockSpec(memory_space=pltpu.VMEM)
    hbm = pl.BlockSpec(memory_space=pltpu.HBM)
    dma = pltpu.SemaphoreType.DMA
    correlation, average = pl.pallas_call(
        functools.partial(kernel, n, groups),
        out_shape=(
            jax.ShapeDtypeStruct((per, atoms), f32),
            jax.ShapeDtypeStruct((per, 128), f32),
        ),
        in_specs=[pl.BlockSpec(memory_space=pltpu.SMEM), hbm, vmem] + [hbm] * 4,
        out_specs=(vmem, vmem),
        scratch_shapes=[
            pltpu.VMEM((xyz, frames, atoms), bf16),
            pltpu.VMEM((2 * frames, frames), bf16),
            pltpu.VMEM((2 * frames, frames), bf16),
            pltpu.VMEM((LAGS, 2 * frames), bf16),
            pltpu.VMEM((LAGS, 2 * frames), bf16),
            pltpu.VMEM((CHUNKS, xyz, frames, width), bf16),
            pltpu.VMEM((CHUNKS, xyz, 2 * frames, width), f32),
            pltpu.VMEM((CHUNKS, 2, nz, 2, per, width), f32),
            pltpu.VMEM((CHUNKS, nz, 2, per, width), f32),
            pltpu.VMEM((CHUNKS, nz, 2, per, width), f32),
            pltpu.VMEM((CHUNKS, nz - 1, 2, per, width), f32),
            pltpu.VMEM((CHUNKS, 2, per, width), f32),
            pltpu.VMEM((CHUNKS, per, width), f32),
            pltpu.VMEM((2, per + 8, 128), f32),
            pltpu.VMEM((2, groups - 1, per + 8, 128), f32),
            dma((5,)),
            dma((CHUNKS, xyz)), dma((CHUNKS, xyz)),
            dma((CHUNKS,)), dma((CHUNKS,)),
            dma((CHUNKS, nz - 1)), dma((CHUNKS, nz - 1)),
            dma((CHUNKS,)), dma((CHUNKS,)),
            dma((2, groups - 1)), dma((2, groups - 1)),
        ],
        compiler_params=pltpu.CompilerParams(
            collective_id=0, has_side_effects=True, vmem_limit_bytes=63 * 1024 * 1024
        ),
    )(
        valid_frames, jnp.transpose(velocities, (1, 0, 2)), atom_mask[None, :],
        *tables(frames, n),
    )
    return correlation, average[:, 0]


def solution(mesh):
    return jax.shard_map(
        body,
        mesh=mesh,
        in_specs=(P("tm", None, "comp"), P("comp"), P()),
        out_specs=(P("tm", "comp"), P("tm")),
        check_vma=False,
    )
```

```python
import functools
import math

import jax
import jax.numpy as jnp
import numpy as np
from jax import lax
from jax.experimental import pallas as pl
from jax.experimental.pallas import tpu as pltpu
from jax.sharding import PartitionSpec as P

LAGS = 256
CHUNKS = 2
MESH = pl.DeviceIdType.MESH


def split_bf16(table):
    high = table.astype(np.float32).astype(jnp.bfloat16)
    low = (table - high.astype(np.float64)).astype(np.float32).astype(jnp.bfloat16)
    return high, low


@functools.lru_cache
def tables(frame_count, count):
    length = 2 * frame_count
    bins = np.arange(frame_count, dtype=np.int64)[:, None]
    own = np.arange(frame_count, dtype=np.int64)[None, :]
    angle = (((2 * bins + 1) * own) % (2 * length)) * (math.pi / length)
    forward = np.concatenate([np.cos(angle), np.sin(angle)], 0)
    per = LAGS // count
    lags = np.arange(LAGS, dtype=np.int64).reshape(count // 4, 2, 2, per)
    lags = lags.transpose(2, 0, 1, 3).reshape(LAGS, 1)
    angle = (((2 * bins.T + 1) * lags) % (2 * length)) * (math.pi / length)
    inverse = np.concatenate([np.cos(angle), -np.sin(angle)], 1) * (2.0 / length)
    return split_bf16(forward) + split_bf16(inverse)


def dot(a, b):
    return jnp.dot(a, b, preferred_element_type=jnp.float32)


def kernel(
    n, groups,
    valid_ref, vel_hbm, mask_ref, fwd_hi_hbm, fwd_lo_hbm, inv_hi_hbm, inv_lo_hbm,
    corr_ref, avg_ref,
    vel_ref, fwd_hi, fwd_lo, inv_hi, inv_lo,
    nxt, spec, part, pair_in, q_ref, z_in, r_ref, x_in, comp_out, comp_in,
    load_s, halo_s, halo_r, pair_s, pair_r, z_s, z_r, x_s, x_r, comp_s, comp_r,
):
    xyz, frames, atoms = vel_ref.shape
    width = atoms // CHUNKS
    nz = n // 4
    per = LAGS // n
    me = lax.axis_index("tm")
    mine = lax.axis_index("comp")
    core = lax.rem(me, 2)
    xpos = lax.rem(me // 2, 2)
    zpos = me // 4
    pair = me + 1 - 2 * core
    across = me + 2 - 4 * xpos
    left = lax.rem(me + n - 1, n)
    right = lax.rem(me + 1, n)

    loads = [
        pltpu.make_async_copy(src, dst, load_s.at[i])
        for i, (src, dst) in enumerate(
            [
                (fwd_hi_hbm, fwd_hi), (fwd_lo_hbm, fwd_lo), (vel_hbm, vel_ref),
                (inv_hi_hbm, inv_hi), (inv_lo_hbm, inv_lo),
            ]
        )
    ]
    for load in loads:
        load.start()

    def along_z(d):
        return lax.rem(zpos + d, nz)

    def z_device(d):
        return along_z(d) * 4 + lax.rem(me, 4)

    def group(d):
        return lax.rem(mine + d, groups)

    barrier = pltpu.get_barrier_semaphore()
    for device in [left, right, pair, across] + [z_device(d) for d in range(1, nz)]:
        pl.semaphore_signal(barrier, inc=1, device_id={"tm": device}, device_id_type=MESH)
    for d in range(1, groups):
        for device in (me, across):
            pl.semaphore_signal(
                barrier, inc=1, device_id={"comp": group(d), "tm": device}, device_id_type=MESH
            )
    pl.semaphore_wait(barrier, 4 + (nz - 1) + 2 * (groups - 1))

    def remote(src, dst, send, recv, device):
        return pltpu.make_async_remote_copy(
            src_ref=src, dst_ref=dst, send_sem=send, recv_sem=recv,
            device_id=device, device_id_type=MESH,
        )

    def halo(c, k):
        lanes = pl.ds(c * width, width)
        return remote(
            vel_hbm.at[k, :, lanes], nxt.at[c, k], halo_s.at[c, k], halo_r.at[c, k], {"tm": left}
        )

    @pl.when(me > 0)
    def _():
        for c in range(CHUNKS):
            for k in range(xyz):
                halo(c, k).start()

    @pl.when(me == n - 1)
    def _():
        nxt[...] = jnp.zeros_like(nxt)

    last_valid = valid_ref[0]

    def keep(offset, lanes):
        row = lax.broadcasted_iota(jnp.int32, (frames, lanes), 0) + (me * frames + offset)
        return jnp.where(row < last_valid, 1.0, 0.0).astype(jnp.bfloat16)

    bins = lax.broadcasted_iota(jnp.int32, (frames, width), 0)
    sign = jnp.where(lax.rem(bins, 2) == 0, 1.0, -1.0)
    weight = mask_ref[...].astype(jnp.float32)

    def spectrum(x):
        return dot(fwd_hi[...], x) + dot(fwd_lo[...], x)

    for load in loads[:3]:
        load.wait()
    step = 2 if CHUNKS % 2 == 0 else 1
    keep_own = keep(0, step * width)
    for c in range(0, CHUNKS, step):
        for k in range(xyz):
            both = spectrum(vel_ref[k, :, c * width : (c + step) * width] * keep_own)
            for j in range(step):
                spec[c + j, k] = both[:, j * width : (j + 1) * width]
    for load in loads[3:]:
        load.wait()

    keep_nxt = keep(frames, width)

    def pair_copy(c):
        return remote(part.at[c, 1 - core], pair_in.at[c], pair_s.at[c], pair_r.at[c], {"tm": pair})

    def z_copy(c, d):
        return remote(
            q_ref.at[c, along_z(d)], z_in.at[c, d - 1], z_s.at[c, d - 1], z_r.at[c, d - 1],
            {"tm": z_device(d)},
        )

    def x_copy(c):
        return remote(r_ref.at[c, 1 - xpos], x_in.at[c], x_s.at[c], x_r.at[c], {"tm": across})

    def lanes_of(c):
        return slice(c * width, (c + 1) * width)

    def atom_sum(c, rows):
        return jnp.sum(weight[:, lanes_of(c)] * rows, axis=1, keepdims=True)

    def after_pair(c):
        pair_copy(c).wait_recv()
        q_ref[c] = part[c, core] + pair_in[c]
        for d in range(1, nz):
            z_copy(c, d).start()

    totals = {}

    def after_z(c):
        rows = q_ref[c, zpos]
        for d in range(1, nz):
            z_copy(c, d).wait_recv()
            rows = rows + z_in[c, d - 1]
        r_ref[c] = rows
        x_copy(c).start()
        totals[c] = (atom_sum(c, r_ref[c, xpos]), atom_sum(c, r_ref[c, 1 - xpos]))

    def correlate(c):
        real = imag = 0.0
        for k in range(xyz):
            if k == 1 and c >= 1:
                after_pair(c - 1)
            if k == xyz - 1 and c >= 2:
                after_z(c - 2)

            @pl.when(me < n - 1)
            def _():
                halo(c, k).wait_recv()

            other = spectrum(nxt[c, k] * keep_nxt)
            nc, ns = -sign * other[frames:], sign * other[:frames]
            ac, as_ = spec[c, k, :frames], spec[c, k, frames:]
            real = real + ac * (ac + nc) + as_ * (as_ + ns)
            imag = imag + as_ * nc - ac * ns
        power = jnp.concatenate([real, imag], 0)
        high = power.astype(jnp.bfloat16)
        low = (power - high.astype(jnp.float32)).astype(jnp.bfloat16)
        sums = dot(inv_hi[...], high) + (dot(inv_hi[...], low) + dot(inv_lo[...], high))
        part[c] = sums.reshape(part.shape[1:])
        pair_copy(c).start()

    for c in range(CHUNKS):
        correlate(c)
    after_pair(CHUNKS - 1)
    if CHUNKS > 1:
        after_z(CHUNKS - 2)
    after_z(CHUNKS - 1)

    total = sum(t[0] for t in totals.values())
    beside = sum(t[1] for t in totals.values())
    real_atoms = jnp.sum(weight, axis=1, keepdims=True)
    comp_out[0, :per] = jnp.broadcast_to(total, (per, 128))
    comp_out[0, per:] = jnp.broadcast_to(real_atoms, (8, 128))
    comp_out[1, :per] = jnp.broadcast_to(beside, (per, 128))
    comp_out[1, per:] = jnp.zeros((8, 128), jnp.float32)

    def comp_copy(side, d):
        return remote(
            comp_out.at[side], comp_in.at[side, d - 1], comp_s.at[side, d - 1],
            comp_r.at[side, d - 1], {"comp": group(d), "tm": (me, across)[side]},
        )

    for side in range(2):
        for d in range(1, groups):
            comp_copy(side, d).start()

    lag = me * per + lax.broadcasted_iota(jnp.int32, (per, width), 0)
    anchors = (last_valid - lag).astype(jnp.float32)
    for c in range(CHUNKS):
        kept = r_ref[c, xpos]
        x_copy(c).wait_recv()
        arrived = x_in[c]
        corr_ref[:, lanes_of(c)] = weight[:, lanes_of(c)] * (kept + arrived) / anchors
        total = total + atom_sum(c, arrived)
    sums = jnp.broadcast_to(total, (per, 128))
    count = jnp.broadcast_to(real_atoms, (8, 128))
    for side in range(2):
        for d in range(1, groups):
            comp_copy(side, d).wait_recv()
            sums = sums + comp_in[side, d - 1, :per]
            count = count + comp_in[side, d - 1, per:]
    avg_ref[...] = sums / anchors[:, :128] / jnp.maximum(count[:1], 1.0)

    @pl.when(me > 0)
    def _():
        for c in range(CHUNKS):
            for k in range(xyz):
                halo(c, k).wait_send()

    for c in range(CHUNKS):
        pair_copy(c).wait_send()
        x_copy(c).wait_send()
        for d in range(1, nz):
            z_copy(c, d).wait_send()
    for side in range(2):
        for d in range(1, groups):
            comp_copy(side, d).wait_send()


def body(velocities, atom_mask, valid_frames):
    frames, xyz, atoms = velocities.shape
    n = lax.axis_size("tm")
    groups = lax.axis_size("comp")
    nz, per, width = n // 4, LAGS // n, atoms // CHUNKS
    f32, bf16 = jnp.float32, jnp.bfloat16
    vmem = pl.BlockSpec(memory_space=pltpu.VMEM)
    hbm = pl.BlockSpec(memory_space=pltpu.HBM)
    dma = pltpu.SemaphoreType.DMA
    correlation, average = pl.pallas_call(
        functools.partial(kernel, n, groups),
        out_shape=(
            jax.ShapeDtypeStruct((per, atoms), f32),
            jax.ShapeDtypeStruct((per, 128), f32),
        ),
        in_specs=[pl.BlockSpec(memory_space=pltpu.SMEM), hbm, vmem] + [hbm] * 4,
        out_specs=(vmem, vmem),
        scratch_shapes=[
            pltpu.VMEM((xyz, frames, atoms), bf16),
            pltpu.VMEM((2 * frames, frames), bf16),
            pltpu.VMEM((2 * frames, frames), bf16),
            pltpu.VMEM((LAGS, 2 * frames), bf16),
            pltpu.VMEM((LAGS, 2 * frames), bf16),
            pltpu.VMEM((CHUNKS, xyz, frames, width), bf16),
            pltpu.VMEM((CHUNKS, xyz, 2 * frames, width), f32),
            pltpu.VMEM((CHUNKS, 2, nz, 2, per, width), f32),
            pltpu.VMEM((CHUNKS, nz, 2, per, width), f32),
            pltpu.VMEM((CHUNKS, nz, 2, per, width), f32),
            pltpu.VMEM((CHUNKS, nz - 1, 2, per, width), f32),
            pltpu.VMEM((CHUNKS, 2, per, width), f32),
            pltpu.VMEM((CHUNKS, per, width), f32),
            pltpu.VMEM((2, per + 8, 128), f32),
            pltpu.VMEM((2, groups - 1, per + 8, 128), f32),
            dma((5,)),
            dma((CHUNKS, xyz)), dma((CHUNKS, xyz)),
            dma((CHUNKS,)), dma((CHUNKS,)),
            dma((CHUNKS, nz - 1)), dma((CHUNKS, nz - 1)),
            dma((CHUNKS,)), dma((CHUNKS,)),
            dma((2, groups - 1)), dma((2, groups - 1)),
        ],
        compiler_params=pltpu.CompilerParams(
            collective_id=0, has_side_effects=True, vmem_limit_bytes=56_500_000
        ),
    )(
        valid_frames, jnp.transpose(velocities, (1, 0, 2)), atom_mask[None, :],
        *tables(frames, n),
    )
    return correlation, average[:, 0]


def solution(mesh):
    return jax.shard_map(
        body,
        mesh=mesh,
        in_specs=(P("tm", None, "comp"), P("comp"), P()),
        out_specs=(P("tm", "comp"), P("tm")),
        check_vma=False,
    )
```

```python
import functools
import math

import jax
import jax.numpy as jnp
import numpy as np
from jax import lax
from jax.experimental import pallas as pl
from jax.experimental.pallas import tpu as pltpu
from jax.sharding import PartitionSpec as P

LAGS = 256
CHUNKS = 2
MESH = pl.DeviceIdType.MESH


def split_bf16(table):
    high = table.astype(np.float32).astype(jnp.bfloat16)
    low = (table - high.astype(np.float64)).astype(np.float32).astype(jnp.bfloat16)
    return high, low


@functools.lru_cache
def tables(frame_count, count):
    length = 2 * frame_count
    bins = np.arange(frame_count, dtype=np.int64)[:, None]
    own = np.arange(frame_count, dtype=np.int64)[None, :]
    angle = (((2 * bins + 1) * own) % (2 * length)) * (math.pi / length)
    forward = np.concatenate([np.cos(angle), np.sin(angle)], 0)
    per = LAGS // count
    lags = np.arange(LAGS, dtype=np.int64).reshape(count // 4, 2, 2, per)
    lags = lags.transpose(2, 0, 1, 3).reshape(LAGS, 1)
    angle = (((2 * bins.T + 1) * lags) % (2 * length)) * (math.pi / length)
    inverse = np.concatenate([np.cos(angle), -np.sin(angle)], 1) * (2.0 / length)
    return split_bf16(forward) + split_bf16(inverse)


def dot(a, b):
    return jnp.dot(a, b, preferred_element_type=jnp.float32)


def kernel(
    n, groups,
    valid_ref, vel_hbm, mask_hbm, fwd_hi_hbm, fwd_lo_hbm, inv_hi_hbm, inv_lo_hbm,
    corr_ref, avg_ref,
    vel_ref, mask_ref, fwd_hi, fwd_lo, inv_hi, inv_lo,
    nxt, spec, part, pair_in, q_ref, z_in, r_ref, x_in, comp_out, comp_in,
    load_s, halo_s, halo_r, pair_s, pair_r, z_s, z_r, x_s, x_r, comp_s, comp_r,
):
    xyz, frames, atoms = vel_ref.shape
    width = atoms // CHUNKS
    nz = n // 4
    per = LAGS // n
    me = lax.axis_index("tm")
    mine = lax.axis_index("comp")
    core = lax.rem(me, 2)
    xpos = lax.rem(me // 2, 2)
    zpos = me // 4
    pair = me + 1 - 2 * core
    across = me + 2 - 4 * xpos
    left = lax.rem(me + n - 1, n)
    right = lax.rem(me + 1, n)

    loads = [
        pltpu.make_async_copy(src, dst, load_s.at[i])
        for i, (src, dst) in enumerate(
            [
                (fwd_hi_hbm, fwd_hi), (fwd_lo_hbm, fwd_lo), (vel_hbm, vel_ref),
                (inv_hi_hbm, inv_hi), (inv_lo_hbm, inv_lo), (mask_hbm, mask_ref),
            ]
        )
    ]
    for load in loads:
        load.start()

    def along_z(d):
        return lax.rem(zpos + d, nz)

    def z_device(d):
        return along_z(d) * 4 + lax.rem(me, 4)

    def group(d):
        return lax.rem(mine + d, groups)

    barrier = pltpu.get_barrier_semaphore()
    for device in [left, right, pair, across] + [z_device(d) for d in range(1, nz)]:
        pl.semaphore_signal(barrier, inc=1, device_id={"tm": device}, device_id_type=MESH)
    for d in range(1, groups):
        for device in (me, across):
            pl.semaphore_signal(
                barrier, inc=1, device_id={"comp": group(d), "tm": device}, device_id_type=MESH
            )
    pl.semaphore_wait(barrier, 4 + (nz - 1) + 2 * (groups - 1))

    def remote(src, dst, send, recv, device):
        return pltpu.make_async_remote_copy(
            src_ref=src, dst_ref=dst, send_sem=send, recv_sem=recv,
            device_id=device, device_id_type=MESH,
        )

    def halo(c, k):
        lanes = pl.ds(c * width, width)
        return remote(
            vel_hbm.at[k, :, lanes], nxt.at[c, k], halo_s.at[c, k], halo_r.at[c, k], {"tm": left}
        )

    @pl.when(me > 0)
    def _():
        for c in range(CHUNKS):
            for k in range(xyz):
                halo(c, k).start()

    @pl.when(me == n - 1)
    def _():
        nxt[...] = jnp.zeros_like(nxt)

    last_valid = valid_ref[0]

    def keep(offset, lanes):
        row = lax.broadcasted_iota(jnp.int32, (frames, lanes), 0) + (me * frames + offset)
        return jnp.where(row < last_valid, 1.0, 0.0).astype(jnp.bfloat16)

    bins = lax.broadcasted_iota(jnp.int32, (frames, width), 0)
    sign = jnp.where(lax.rem(bins, 2) == 0, 1.0, -1.0)

    def spectrum(x):
        return dot(fwd_hi[...], x) + dot(fwd_lo[...], x)

    for load in loads[:3]:
        load.wait()
    step = 2 if CHUNKS % 2 == 0 else 1
    keep_own = keep(0, step * width)
    for c in range(0, CHUNKS, step):
        for k in range(xyz):
            both = spectrum(vel_ref[k, :, c * width : (c + step) * width] * keep_own)
            for j in range(step):
                spec[c + j, k] = both[:, j * width : (j + 1) * width]
    for load in loads[3:]:
        load.wait()
    weight = mask_ref[...].astype(jnp.float32)

    keep_nxt = keep(frames, width)

    def pair_copy(c):
        return remote(part.at[c, 1 - core], pair_in.at[c], pair_s.at[c], pair_r.at[c], {"tm": pair})

    def z_copy(c, d):
        return remote(
            q_ref.at[c, along_z(d)], z_in.at[c, d - 1], z_s.at[c, d - 1], z_r.at[c, d - 1],
            {"tm": z_device(d)},
        )

    def x_copy(c):
        return remote(r_ref.at[c, 1 - xpos], x_in.at[c], x_s.at[c], x_r.at[c], {"tm": across})

    def lanes_of(c):
        return slice(c * width, (c + 1) * width)

    def atom_sum(c, rows):
        return jnp.sum(weight[:, lanes_of(c)] * rows, axis=1, keepdims=True)

    def after_pair(c):
        pair_copy(c).wait_recv()
        q_ref[c] = part[c, core] + pair_in[c]
        for d in range(1, nz):
            z_copy(c, d).start()

    totals = {}

    def after_z(c):
        rows = q_ref[c, zpos]
        for d in range(1, nz):
            z_copy(c, d).wait_recv()
            rows = rows + z_in[c, d - 1]
        r_ref[c] = rows
        x_copy(c).start()
        totals[c] = (atom_sum(c, r_ref[c, xpos]), atom_sum(c, r_ref[c, 1 - xpos]))

    def correlate(c):
        real = imag = 0.0
        for k in range(xyz):
            if k == 1 and c >= 1:
                after_pair(c - 1)
            if k == xyz - 1 and c >= 2:
                after_z(c - 2)

            @pl.when(me < n - 1)
            def _():
                halo(c, k).wait_recv()

            other = spectrum(nxt[c, k] * keep_nxt)
            nc, ns = -sign * other[frames:], sign * other[:frames]
            ac, as_ = spec[c, k, :frames], spec[c, k, frames:]
            real = real + ac * (ac + nc) + as_ * (as_ + ns)
            imag = imag + as_ * nc - ac * ns
        power = jnp.concatenate([real, imag], 0)
        high = power.astype(jnp.bfloat16)
        low = (power - high.astype(jnp.float32)).astype(jnp.bfloat16)
        sums = dot(inv_hi[...], high) + (dot(inv_hi[...], low) + dot(inv_lo[...], high))
        part[c] = sums.reshape(part.shape[1:])
        pair_copy(c).start()

    for c in range(CHUNKS):
        correlate(c)
    after_pair(CHUNKS - 1)
    if CHUNKS > 1:
        after_z(CHUNKS - 2)
    after_z(CHUNKS - 1)

    total = sum(t[0] for t in totals.values())
    beside = sum(t[1] for t in totals.values())
    real_atoms = jnp.sum(weight, axis=1, keepdims=True)
    comp_out[0, :per] = jnp.broadcast_to(total, (per, 128))
    comp_out[0, per:] = jnp.broadcast_to(real_atoms, (8, 128))
    comp_out[1, :per] = jnp.broadcast_to(beside, (per, 128))
    comp_out[1, per:] = jnp.zeros((8, 128), jnp.float32)

    def comp_copy(side, d):
        return remote(
            comp_out.at[side], comp_in.at[side, d - 1], comp_s.at[side, d - 1],
            comp_r.at[side, d - 1], {"comp": group(d), "tm": (me, across)[side]},
        )

    for side in range(2):
        for d in range(1, groups):
            comp_copy(side, d).start()

    lag = me * per + lax.broadcasted_iota(jnp.int32, (per, width), 0)
    anchors = (last_valid - lag).astype(jnp.float32)
    for c in range(CHUNKS):
        kept = r_ref[c, xpos]
        x_copy(c).wait_recv()
        arrived = x_in[c]
        corr_ref[:, lanes_of(c)] = weight[:, lanes_of(c)] * (kept + arrived) / anchors
        total = total + atom_sum(c, arrived)
    sums = jnp.broadcast_to(total, (per, 128))
    count = jnp.broadcast_to(real_atoms, (8, 128))
    for side in range(2):
        for d in range(1, groups):
            comp_copy(side, d).wait_recv()
            sums = sums + comp_in[side, d - 1, :per]
            count = count + comp_in[side, d - 1, per:]
    avg_ref[...] = sums / anchors[:, :128] / jnp.maximum(count[:1], 1.0)

    @pl.when(me > 0)
    def _():
        for c in range(CHUNKS):
            for k in range(xyz):
                halo(c, k).wait_send()

    for c in range(CHUNKS):
        pair_copy(c).wait_send()
        x_copy(c).wait_send()
        for d in range(1, nz):
            z_copy(c, d).wait_send()
    for side in range(2):
        for d in range(1, groups):
            comp_copy(side, d).wait_send()


def body(velocities, atom_mask, valid_frames):
    frames, xyz, atoms = velocities.shape
    n = lax.axis_size("tm")
    groups = lax.axis_size("comp")
    nz, per, width = n // 4, LAGS // n, atoms // CHUNKS
    f32, bf16 = jnp.float32, jnp.bfloat16
    vmem = pl.BlockSpec(memory_space=pltpu.VMEM)
    hbm = pl.BlockSpec(memory_space=pltpu.HBM)
    dma = pltpu.SemaphoreType.DMA
    correlation, average = pl.pallas_call(
        functools.partial(kernel, n, groups),
        out_shape=(
            jax.ShapeDtypeStruct((per, atoms), f32),
            jax.ShapeDtypeStruct((per, 128), f32),
        ),
        in_specs=[pl.BlockSpec(memory_space=pltpu.SMEM)] + [hbm] * 6,
        out_specs=(vmem, vmem),
        scratch_shapes=[
            pltpu.VMEM((xyz, frames, atoms), bf16),
            pltpu.VMEM((1, atoms), jnp.int32),
            pltpu.VMEM((2 * frames, frames), bf16),
            pltpu.VMEM((2 * frames, frames), bf16),
            pltpu.VMEM((LAGS, 2 * frames), bf16),
            pltpu.VMEM((LAGS, 2 * frames), bf16),
            pltpu.VMEM((CHUNKS, xyz, frames, width), bf16),
            pltpu.VMEM((CHUNKS, xyz, 2 * frames, width), f32),
            pltpu.VMEM((CHUNKS, 2, nz, 2, per, width), f32),
            pltpu.VMEM((CHUNKS, nz, 2, per, width), f32),
            pltpu.VMEM((CHUNKS, nz, 2, per, width), f32),
            pltpu.VMEM((CHUNKS, nz - 1, 2, per, width), f32),
            pltpu.VMEM((CHUNKS, 2, per, width), f32),
            pltpu.VMEM((CHUNKS, per, width), f32),
            pltpu.VMEM((2, per + 8, 128), f32),
            pltpu.VMEM((2, groups - 1, per + 8, 128), f32),
            dma((6,)),
            dma((CHUNKS, xyz)), dma((CHUNKS, xyz)),
            dma((CHUNKS,)), dma((CHUNKS,)),
            dma((CHUNKS, nz - 1)), dma((CHUNKS, nz - 1)),
            dma((CHUNKS,)), dma((CHUNKS,)),
            dma((2, groups - 1)), dma((2, groups - 1)),
        ],
        compiler_params=pltpu.CompilerParams(
            collective_id=0, has_side_effects=True, vmem_limit_bytes=56_500_000
        ),
    )(
        valid_frames, jnp.transpose(velocities, (1, 0, 2)), atom_mask[None, :],
        *tables(frames, n),
    )
    return correlation, average[:, 0]


def solution(mesh):
    return jax.shard_map(
        body,
        mesh=mesh,
        in_specs=(P("tm", None, "comp"), P("comp"), P()),
        out_specs=(P("tm", "comp"), P("tm")),
        check_vma=False,
    )
```
